32 devices in a mesh: seq: 16 (over z, y, core), head: 2 (over x).
Axes of the slice: x: 2, y: 2, z: 4, core: 2. Of those that a mesh axis runs over, the one named last changes fastest.
Arguments:
- states: bfloat16 [4096, 4096], P('seq', 'head'), may hold values from -6 to 6
- queries: bfloat16 [4096, 4096], P('seq', 'head'), may hold values from -240 to 240
- w_key: bfloat16 [4096, 1024], P('seq', 'head'), may hold values from -0.09375 to 0.09375
- w_value: bfloat16 [4096, 1024], P('seq', 'head'), may hold values from -0.09375 to 0.09375
- grad_out: bfloat16 [4096, 4096], P('seq', 'head'), may hold values from -6 to 6
- lengths: int32 [16, 4], replicated, may hold values from 16 to 208, as said below
- give_plan: int32 [16], replicated, may hold values from 0 to 128, as said below
Outputs:
- attended: bfloat16 [6144, 4096], P('seq', 'head')
- query_grad: bfloat16 [6144, 4096], P('seq', 'head')
- key_weight_grad: float32 [4096, 1024], P('seq', 'head')
- value_weight_grad: float32 [4096, 1024], P('seq', 'head')
The draws below stay inside these ranges and needn't reach their ends.
Inputs may be any that keep to these rules, and one draw needn't show every extreme that they name: Each row holds 4 lengths, multiples of 16, summing to 256. give_plan[s] is 0 or 128; where it is 128, shard s's trailing documents fill exactly its last 128 tokens. Some shard gives in every draw.
All inputs are finite; a program needn't handle non-finite values.
Results may differ from the reference program's by a relative error of at most 0.023.
The reference program's roundings to bfloat16 on the way count: a program that leaves them out, or rounds other values in their place, can miss the bound.
Values may be sent and summed in bfloat16 or wider, within the bound.
A program may use at most 64 MiB of HBM per device.

```python
import jax
import jax.numpy as jnp
from jax import lax

D = 4096
QH = 32
KVH = 8
HD = 128
GROUP = 4
TOK_DEV = 256
GIVE = 128
DOCS_DEV = 4
SHARDS = 16
TOKENS = 4096
SLAB = 384


granule = 16


def layout(key):
    base = jax.random.fold_in(key, 11)
    subkeys = jax.random.split(base, 4)
    half_count = SHARDS // 2
    shard_ids = jnp.arange(SHARDS, dtype=jnp.int32)
    heavy = jax.random.randint(subkeys[0], (SHARDS,), 0, 2).astype(jnp.int32)
    forced = (shard_ids == 0) | (shard_ids == half_count - 1) | (shard_ids == half_count) | (shard_ids == SHARDS - 1)
    heavy = jnp.where(forced, 1, heavy)
    heavy = jnp.where(shard_ids == 1, 0, heavy)
    light_slots = TOK_DEV // granule - 1
    heavy_slots = (TOK_DEV - GIVE) // granule - 1

    def light_shuffle(subkey):
        return jax.random.permutation(subkey, light_slots).astype(jnp.int32)

    def heavy_shuffle(subkey):
        return jax.random.permutation(subkey, heavy_slots).astype(jnp.int32)
    light_perm = jax.vmap(light_shuffle)(jax.random.split(subkeys[2], SHARDS))
    heavy_perm = jax.vmap(heavy_shuffle)(jax.random.split(subkeys[3], SHARDS))
    light_cuts = jnp.sort(light_perm[:, :DOCS_DEV - 1], axis=1) + 1
    packed_cuts = jnp.arange(1, DOCS_DEV, dtype=jnp.int32)[None, :]
    light_cuts = jnp.where(shard_ids[:, None] == 1, packed_cuts, light_cuts)
    heavy_fixed = jnp.full((SHARDS, 1), (TOK_DEV - GIVE) // granule, jnp.int32)
    heavy_cuts = jnp.concatenate([jnp.sort(heavy_perm[:, :DOCS_DEV - 2], axis=1) + 1, heavy_fixed], axis=1)
    cuts = jnp.where(heavy[:, None] == 1, heavy_cuts, light_cuts) * granule
    bounds = jnp.concatenate([jnp.zeros((SHARDS, 1), jnp.int32), cuts.astype(jnp.int32), jnp.full((SHARDS, 1), TOK_DEV, jnp.int32)], axis=1)
    lengths = bounds[:, 1:] - bounds[:, :-1]
    gives = jnp.where(heavy == 1, GIVE, 0)
    return (lengths.astype(jnp.int32), gives.astype(jnp.int32))


def draw_lengths(key, part):
    return layout(key)[0]


def draw_give_plan(key, part):
    return layout(key)[1]


def draw_queries(key, part):
    samples = jax.random.normal(jax.random.fold_in(key, 3), (TOKENS, QH * HD), jnp.float32)
    return jnp.clip(samples, -240.0, 240.0).astype(jnp.bfloat16)


def spiked(result, key, source, target, shards_of, factor):
    def block_of(position):
        return (jnp.arange(result.shape[position]) // (result.shape[position] // shards_of)).reshape((-1,) + (1,) * (result.ndim - 1 - position))

    first = jax.random.permutation(key, shards_of)[block_of(target)]
    far = (block_of(target) + shards_of // 2) % shards_of
    return jnp.where((block_of(source) == first) | (block_of(source) == far), factor * result, result)


def steps_of(rng, extent, cuts, smallest, largest):
    def one(position, parts):
        draws = jax.random.uniform(jax.random.fold_in(jax.random.fold_in(rng, 6), position), (parts,), jnp.float32, smallest / len(cuts), largest / len(cuts))
        return jnp.repeat(jnp.exp(draws), extent[position] // parts).reshape((-1,) + (1,) * (len(extent) - position - 1))

    factor_of = one(*cuts[0])
    for cut in cuts[1:]:
        factor_of = factor_of * one(*cut)
    return factor_of


def noise(key, dims, scale, limit, cuts=(), kind=jnp.bfloat16):
    array = jax.random.normal(key, dims, jnp.float32) * scale
    if len(cuts) > 0:
        array = steps_of(key, dims, cuts, -0.22, 0.18) * array
    return jnp.clip(array, min=-limit, max=limit).astype(kind)


def gaussian_with(rng, extent, width, most, cuts, heavy, kind=jnp.bfloat16):
    drawn = width * jax.random.normal(rng, extent, jnp.float32)
    if cuts:
        drawn = drawn * steps_of(rng, extent, cuts, -0.22, 0.18)
    return jnp.clip(spiked(drawn, jax.random.fold_in(rng, 3), *heavy), -most, most).astype(kind)


def setup_inputs(seed: int = 0) -> dict:
    key_list = jax.random.split(jax.random.key(seed), 8)
    states = gaussian_with(key_list[0], (TOKENS, D), 1.0, 6.0, ((0, 16), (1, 2)), (0, 1, 16, 2.0))
    queries = draw_queries(jax.random.fold_in(key_list[7], 71), 0)
    w_key = noise(key_list[2], (D, KVH * HD), D ** -0.5, 0.09375, ((0, 16), (1, 2)))
    w_value = noise(key_list[3], (D, KVH * HD), D ** -0.5, 0.09375, ((0, 16), (1, 2)))
    grad_out = noise(key_list[4], (TOKENS, QH * HD), 1.0, 6.0, ((0, 16), (1, 2)))
    lengths = draw_lengths(jax.random.fold_in(key_list[7], 71), 0)
    give_plan = draw_give_plan(jax.random.fold_in(key_list[7], 71), 0)
    return dict(states=states, queries=queries, w_key=w_key, w_value=w_value, grad_out=grad_out, lengths=lengths, give_plan=give_plan)


def document_ids(lengths):
    doc_ends = jnp.cumsum(lengths, axis=1)
    places = jnp.arange(TOK_DEV, dtype=jnp.int32)
    return jnp.sum((places[None, :, None] >= doc_ends[:, None, :]).astype(jnp.int32), axis=2)


def attend(queries, keys, values, grad_out, segment):
    row_count = queries.shape[0]
    score_scale = HD ** -0.5
    query_heads = queries.astype(jnp.float32).reshape(row_count, KVH, GROUP, HD)
    key_heads = keys.astype(jnp.float32).reshape(row_count, KVH, HD)
    value_heads = values.astype(jnp.float32).reshape(row_count, KVH, HD)
    grad_heads = grad_out.astype(jnp.float32).reshape(row_count, KVH, GROUP, HD)
    scores = jnp.einsum("tkgd,ukd->kgtu", query_heads, key_heads) * score_scale
    places = jnp.arange(row_count, dtype=jnp.int32)
    allowed = (segment[:, None] == segment[None, :]) & (places[None, :] <= places[:, None])
    scores = jnp.where(allowed, scores, jnp.float32(-1e30))
    row_max = jnp.max(scores, axis=-1, keepdims=True)
    exponent = jnp.exp(scores - row_max)
    soft_weights = exponent / jnp.sum(exponent, axis=-1, keepdims=True)
    soft_rounded = lax.optimization_barrier(soft_weights.astype(jnp.bfloat16)).astype(jnp.float32)
    attended = jnp.einsum("kgtu,ukd->tkgd", soft_rounded, value_heads).astype(jnp.bfloat16)
    attended_wide = lax.optimization_barrier(attended).astype(jnp.float32)
    grad_probs = jnp.einsum("tkgd,ukd->kgtu", grad_heads, value_heads)
    row_dots = jnp.einsum("tkgd,tkgd->kgt", grad_heads, attended_wide)
    grad_scores = (soft_weights * (grad_probs - row_dots[..., None])).astype(jnp.bfloat16)
    grad_scores = lax.optimization_barrier(grad_scores).astype(jnp.float32)
    query_grad = (jnp.einsum("kgtu,ukd->tkgd", grad_scores, key_heads) * score_scale).astype(jnp.bfloat16)
    key_grad = (jnp.einsum("kgtu,tkgd->ukd", grad_scores, query_heads) * score_scale).astype(jnp.bfloat16)
    value_grad = jnp.einsum("kgtu,tkgd->ukd", soft_rounded, grad_heads).astype(jnp.bfloat16)
    return (attended.reshape(row_count, KVH * GROUP * HD), query_grad.reshape(row_count, KVH * GROUP * HD),
            key_grad.reshape(row_count, KVH * HD), value_grad.reshape(row_count, KVH * HD))


def rebalance(blocks, give_plan):
    shard_ids = jnp.arange(SHARDS, dtype=jnp.int32)
    partners = jnp.bitwise_xor(shard_ids, SHARDS // 2)
    places = jnp.arange(TOK_DEV, dtype=jnp.int32)
    kept = jnp.where((places[None, :] < TOK_DEV - give_plan[:, None])[:, :, None], blocks, jnp.zeros_like(blocks))
    tails = blocks[partners][:, TOK_DEV - GIVE:, :]
    slots = jnp.arange(GIVE, dtype=jnp.int32)
    taken = jnp.where((slots[None, :] >= GIVE - give_plan[partners][:, None])[:, :, None], tails, jnp.zeros_like(tails))
    return jnp.concatenate([kept, taken], axis=1).reshape(SHARDS * SLAB, blocks.shape[2])


def reference(states, queries, w_key, w_value, grad_out, lengths, give_plan):
    keys = jnp.dot(states, w_key, preferred_element_type=jnp.float32).astype(jnp.bfloat16)
    values = jnp.dot(states, w_value, preferred_element_type=jnp.float32).astype(jnp.bfloat16)
    segments = document_ids(lengths)

    def per_shard(pieces):
        return attend(pieces[0], pieces[1], pieces[2], pieces[3], pieces[4])

    shaped = (queries.reshape(SHARDS, TOK_DEV, QH * HD), keys.reshape(SHARDS, TOK_DEV, KVH * HD),
              values.reshape(SHARDS, TOK_DEV, KVH * HD), grad_out.reshape(SHARDS, TOK_DEV, QH * HD), segments)
    attended, query_grad, key_grad, value_grad = lax.map(per_shard, shaped)
    key_weight_grad = jnp.dot(states.T, key_grad.reshape(TOKENS, KVH * HD), preferred_element_type=jnp.float32)
    value_weight_grad = jnp.dot(states.T, value_grad.reshape(TOKENS, KVH * HD), preferred_element_type=jnp.float32)
    return (rebalance(attended, give_plan), rebalance(query_grad, give_plan), key_weight_grad, value_weight_grad)
```

```python
import functools

import jax
import jax.numpy as jnp
from jax import lax
from jax.experimental import pallas as pl
from jax.experimental.pallas import tpu as pltpu
from jax.sharding import PartitionSpec as P

HD = 128
GROUP = 4
GIVE = 128
QUAD = 4
MESH = pl.DeviceIdType.MESH
F32 = jnp.float32
BF16 = jnp.bfloat16


def greet(peers):
    barrier = pltpu.get_barrier_semaphore()
    for peer in peers:
        pl.semaphore_signal(barrier, inc=1, device_id=peer, device_id_type=MESH)
    pl.semaphore_wait(barrier, len(peers))


def remote(src, dst, send, recv, device):
    return pltpu.make_async_remote_copy(
        src_ref=src, dst_ref=dst, send_sem=send, recv_sem=recv, device_id=device, device_id_type=MESH
    )


def project_kernel(
    chain, heads,
    st_ref, wk_ref, wv_ref,
    keys_ref, values_ref, turned_ref,
    st_all, w_all, acc,
    st_send, st_recv, z_send, z_recv, y_send, y_recv, c_send, c_recv, own_sem, st_own_sem,
):
    seq = lax.axis_index("seq")
    head = lax.axis_index("head")
    z, quad = seq // QUAD, seq % QUAD
    base = z * QUAD
    other_y = base + (quad + 2) % 4
    other_c = base + (quad // 2) * 2 + (quad + 1) % 2
    rows, cols = wk_ref.shape
    wide = QUAD * rows
    pieces = st_ref.shape[1] // wide
    z_peers = [((z + k) % chain) * QUAD + quad for k in range(1, chain)]
    h_peers = [(head + k) % heads for k in range(1, heads)]
    greet(
        [(p, head) for p in z_peers] + [(other_y, head), (other_c, head)] + [(seq, p) for p in h_peers]
    )

    def rows_of(zz, qq):
        return pl.ds(pl.multiple_of((zz * QUAD + qq) * rows, rows), rows)

    def half(ref, at, side):
        return ref.at[at, pl.ds(side * cols, cols)]

    mine = rows_of(z, quad)
    sent = []

    def go(copy):
        copy.start()
        sent.append(copy)

    for side, src in ((0, wk_ref), (1, wv_ref)):
        go(remote(src, half(w_all, mine, side), y_send.at[0, side], y_recv.at[0, side], (other_y, head)))
        for k in range(1, chain):
            go(remote(src, half(w_all, mine, side), z_send.at[k, side], z_recv.at[k, side], (z_peers[k - 1], head)))
        go(remote(src, half(w_all, mine, side), c_send.at[0, 0, side], c_recv.at[0, 0, side], (other_c, head)))
    own = []
    for n in range(pieces):
        part = st_ref.at[:, pl.ds(n * wide, wide)]
        for k in range(1, heads):
            go(remote(part, st_all.at[head * pieces + n], st_send.at[k, n], st_recv.at[k, n], (seq, h_peers[k - 1])))
        own.append(pltpu.make_async_copy(part, st_all.at[head * pieces + n], st_own_sem.at[n]))
    for side, src in ((0, wk_ref), (1, wv_ref)):
        own.append(pltpu.make_async_copy(src, half(w_all, mine, side), own_sem.at[side]))
    for copy in own:
        copy.start()
    for copy in own:
        copy.wait()

    def turn(slot):
        flipped = st_all[slot].T
        for q in range(QUAD):
            turned_ref[q, pl.ds(pl.multiple_of(slot * rows, rows), rows), :] = flipped[q * rows:(q + 1) * rows, :]

    for n in range(pieces):
        turn(head * pieces + n)

    def source(k):
        return (z - k + chain) % chain

    def arrive_z(k):
        for side in range(2):
            block = half(w_all, rows_of(source(k), quad), side)
            remote(block, block, z_send.at[k, side], z_recv.at[k, side], (other_y, head)).wait_recv()
            go(remote(block, block, y_send.at[k, side], y_recv.at[k, side], (other_y, head)))
            go(remote(block, block, c_send.at[k, 0, side], c_recv.at[k, 0, side], (other_c, head)))

    def arrive_y(k):
        for side in range(2):
            block = half(w_all, rows_of(source(k), (quad + 2) % 4), side)
            remote(block, block, y_send.at[k, side], y_recv.at[k, side], (other_y, head)).wait_recv()
            go(remote(block, block, c_send.at[k, 1, side], c_recv.at[k, 1, side], (other_c, head)))

    mate = (quad // 2) * 2 + (quad + 1) % 2

    def arrive_c(k):
        for side in range(2):
            for far, qq in ((0, mate), (1, (mate + 2) % 4)):
                block = half(w_all, rows_of(source(k), qq), side)
                remote(
                    block, block, c_send.at[k, far, side], c_recv.at[k, far, side], (other_c, head)
                ).wait_recv()

    tile = min(2 * cols, 256)

    def multiply(k):
        slot = source(k)
        at = pl.ds(pl.multiple_of(slot * wide, wide), wide)

        def step(t, carry):
            where = pl.ds(pl.multiple_of(t * tile, tile), tile)
            term = jnp.dot(st_all[slot], w_all[at, where], preferred_element_type=F32)
            if k == 0:
                acc[:, where] = term
            else:
                acc[:, where] += term
            return carry

        lax.fori_loop(0, 2 * cols // tile, step, 0)

    for k in range(chain):
        if k:
            arrive_z(k)
        if k == 1:
            for m in range(1, heads):
                for n in range(pieces):
                    slot = ((head - m + heads) % heads) * pieces + n
                    dst = st_all.at[slot]
                    remote(dst, dst, st_send.at[m, n], st_recv.at[m, n], (seq, h_peers[m - 1])).wait_recv()
                    turn(slot)
            arrive_y(0)
        elif k > 1:
            arrive_y(k - 1)
            arrive_c(k - 2)
            multiply(k - 2)
    arrive_y(chain - 1)
    arrive_c(chain - 2)
    multiply(chain - 2)
    arrive_c(chain - 1)
    multiply(chain - 1)
    keys_ref[...] = acc[:, :cols].astype(BF16)
    values_ref[...] = acc[:, cols:].astype(BF16)
    for copy in sent:
        copy.wait_send()


def attend_kernel(
    chain,
    turned_ref, q_ref, go_ref, keys_ref, values_ref, seg_row, seg_col,
    att_ref, dq_ref, got_att, got_dq, dwk_ref, dwv_ref,
    group_states, pair, terms, parts, total, whole,
    s_send, s_recv, p_send, p_recv, t_send, t_recv, h_send, h_recv, own_sem,
):
    seq = lax.axis_index("seq")
    head = lax.axis_index("head")
    z, quad = seq // QUAD, seq % QUAD
    base = z * QUAD
    tok = q_ref.shape[0]
    kv = keys_ref.shape[1] // HD
    rows = dwk_ref.shape[0]
    scale = HD ** (-0.5)
    across = ((z + chain // 2) % chain) * QUAD + quad
    z_peers = [((z + k) % chain) * QUAD + quad for k in range(1, chain)]
    quads = [(quad + i) % QUAD for i in range(QUAD)]
    greet([(p, head) for p in z_peers] + [(base + p, head) for p in quads[1:]])

    def span(i):
        return pl.ds(pl.multiple_of(i * tok, tok), tok)

    def states_copy(i):
        return remote(
            turned_ref.at[quads[i]], group_states.at[:, span(quad)],
            s_send.at[i], s_recv.at[i], (base + quads[i], head),
        )

    for i in range(1, QUAD):
        states_copy(i).start()
    own = pltpu.make_async_copy(turned_ref.at[quad], group_states.at[:, span(quad)], own_sem)
    own.start()
    own.wait()

    def pair_copy(g, i):
        return remote(
            pair.at[g, span(quad), :], pair.at[g, span(quad), :],
            p_send.at[g, i], p_recv.at[g, i], (base + quads[i], head),
        )

    def tail_copy(g, which):
        ref, dst = ((att_ref, got_att), (dq_ref, got_dq))[which]
        at = pl.ds(pl.multiple_of(g * (GROUP * HD), GROUP * HD), GROUP * HD)
        return remote(
            ref.at[pl.ds(tok - GIVE, GIVE), at], dst.at[:, at],
            h_send.at[g, which], h_recv.at[g, which], (across, head),
        )

    def term_copy(g, k):
        to = (z + k) % chain
        return remote(
            terms.at[g, pl.ds(pl.multiple_of(to * rows, rows), rows), :], parts.at[k - 1, g],
            t_send.at[g, k - 1], t_recv.at[g, k - 1], (z_peers[k - 1], head),
        )

    places_r = lax.broadcasted_iota(jnp.int32, (tok, tok), 0)
    places_c = lax.broadcasted_iota(jnp.int32, (tok, tok), 1)
    allowed = (seg_row[...] == seg_col[...]) & (places_c <= places_r)
    nt = (((1,), (1,)), ((), ()))
    tn = (((0,), (0,)), ((), ()))

    def attend(g):
        at = pl.ds(pl.multiple_of(g * HD, HD), HD)
        key, value = keys_ref[:, at], values_ref[:, at]
        dk = dv = None
        for m in range(GROUP):
            col = pl.ds(pl.multiple_of(g * (GROUP * HD) + m * HD, HD), HD)
            query, grad = q_ref[:, col], go_ref[:, col]
            scores = lax.dot_general(query, key, nt, preferred_element_type=F32) * scale
            scores = jnp.where(allowed, scores, F32(-1e30))
            top = jnp.max(scores, axis=-1, keepdims=True)
            grown = jnp.exp(scores - top)
            probs = grown / jnp.sum(grown, axis=-1, keepdims=True)
            low = probs.astype(BF16)
            out = jnp.dot(low, value, preferred_element_type=F32).astype(BF16)
            att_ref[:, col] = out
            grad_probs = lax.dot_general(grad, value, nt, preferred_element_type=F32)
            dots = jnp.sum(grad.astype(F32) * out.astype(F32), axis=-1, keepdims=True)
            slope = (probs * (grad_probs - dots)).astype(BF16)
            dq = jnp.dot(slope, key, preferred_element_type=F32) * scale
            dq_ref[:, col] = dq.astype(BF16)
            dk_m = lax.dot_general(slope, query, tn, preferred_element_type=F32)
            dv_m = lax.dot_general(low, grad, tn, preferred_element_type=F32)
            dk = dk_m if dk is None else dk + dk_m
            dv = dv_m if dv is None else dv + dv_m
        pair[g, span(quad), pl.ds(0, HD)] = (dk * scale).astype(BF16)
        pair[g, span(quad), pl.ds(HD, HD)] = dv.astype(BF16)
        for i in range(1, QUAD):
            pair_copy(g, i).start()
        for which in range(2):
            tail_copy(g, which).start()

    def reduce(g):
        for i in range(1, QUAD):
            pair_copy(g, i).wait_recv()
        whole[...] = jnp.dot(group_states[...], pair[g], preferred_element_type=F32)
        terms[g] = whole[...].astype(BF16)
        for k in range(1, chain):
            term_copy(g, k).start()
        total[g] = whole[pl.ds(pl.multiple_of(z * rows, rows), rows), :]

    def step(g, carry):
        @pl.when(g < kv)
        def _():
            attend(g)

        @pl.when(g == 1)
        def _():
            for i in range(1, QUAD):
                states_copy(i).wait_recv()

        @pl.when(g > 0)
        def _():
            reduce(g - 1)

        return carry

    lax.fori_loop(0, kv + 1, step, 0)
    for g in range(kv):
        value = total[g]
        for k in range(1, chain):
            term_copy(g, k).wait_recv()
            value = value + parts[k - 1, g].astype(F32)
        dwk_ref[:, pl.ds(g * HD, HD)] = value[:, :HD]
        dwv_ref[:, pl.ds(g * HD, HD)] = value[:, HD:]
    for g in range(kv):
        for which in range(2):
            tail_copy(g, which).wait()
        for i in range(1, QUAD):
            pair_copy(g, i).wait_send()
        for k in range(1, chain):
            term_copy(g, k).wait_send()
    for i in range(1, QUAD):
        states_copy(i).wait_send()


def segment_ids(row_lengths, row_total):
    doc_ends = jnp.cumsum(row_lengths)
    places = jnp.arange(row_total, dtype=jnp.int32)
    return jnp.sum((places[:, None] >= doc_ends[None, :]).astype(jnp.int32), axis=1)


def local(states, queries, w_key, w_value, grad_out, lengths, give_plan):
    count, heads = lax.axis_size("seq"), lax.axis_size("head")
    chain = count // QUAD
    shard = lax.axis_index("seq")
    partner = jnp.bitwise_xor(shard, count // 2)
    tok = states.shape[0]
    rows, cols = w_key.shape
    kv = cols // HD
    deep = rows * count
    pieces = states.shape[1] // (QUAD * rows)
    vmem = pl.BlockSpec(memory_space=pltpu.VMEM)
    dma = pltpu.SemaphoreType.DMA
    limit = 56 * 2**20
    keys, values, turned = pl.pallas_call(
        functools.partial(project_kernel, chain, heads),
        out_shape=(
            jax.ShapeDtypeStruct((tok, cols), BF16),
            jax.ShapeDtypeStruct((tok, cols), BF16),
            jax.ShapeDtypeStruct((QUAD, chain * rows, tok), BF16),
        ),
        in_specs=[vmem] * 3,
        out_specs=(vmem,) * 3,
        scratch_shapes=[
            pltpu.VMEM((chain, tok, QUAD * rows), BF16),
            pltpu.VMEM((deep, 2 * cols), BF16),
            pltpu.VMEM((tok, 2 * cols), F32),
            dma((heads, pieces)), dma((heads, pieces)),
            dma((chain, 2)), dma((chain, 2)),
            dma((chain, 2)), dma((chain, 2)),
            dma((chain, 2, 2)), dma((chain, 2, 2)),
            dma((2,)), dma((pieces,)),
        ],
        compiler_params=pltpu.CompilerParams(
            collective_id=0, has_side_effects=True, vmem_limit_bytes=limit
        ),
        name="project",
    )(states, w_key, w_value)
    segment = segment_ids(lax.dynamic_index_in_dim(lengths, shard, 0, keepdims=False), tok)
    att, dq, got_att, got_dq, dwk, dwv = pl.pallas_call(
        functools.partial(attend_kernel, chain),
        out_shape=(
            jax.ShapeDtypeStruct(queries.shape, BF16),
            jax.ShapeDtypeStruct(queries.shape, BF16),
            jax.ShapeDtypeStruct((GIVE, queries.shape[1]), BF16),
            jax.ShapeDtypeStruct((GIVE, queries.shape[1]), BF16),
            jax.ShapeDtypeStruct((rows, cols), F32),
            jax.ShapeDtypeStruct((rows, cols), F32),
        ),
        in_specs=[vmem] * 7,
        out_specs=(vmem,) * 6,
        scratch_shapes=[
            pltpu.VMEM((chain * rows, QUAD * tok), BF16),
            pltpu.VMEM((kv, QUAD * tok, 2 * HD), BF16),
            pltpu.VMEM((kv, chain * rows, 2 * HD), BF16),
            pltpu.VMEM((chain - 1, kv, rows, 2 * HD), BF16),
            pltpu.VMEM((kv, rows, 2 * HD), F32),
            pltpu.VMEM((chain * rows, 2 * HD), F32),
            dma((QUAD,)), dma((QUAD,)),
            dma((kv, QUAD)), dma((kv, QUAD)),
            dma((kv, chain - 1)), dma((kv, chain - 1)),
            dma((kv, 2)), dma((kv, 2)),
            dma,
        ],
        compiler_params=pltpu.CompilerParams(
            collective_id=1, has_side_effects=True, vmem_limit_bytes=limit
        ),
        name="attend",
    )(turned, queries, grad_out, keys, values, segment[:, None], segment[None, :])
    own_give = lax.dynamic_index_in_dim(give_plan, shard, 0, keepdims=False)
    other_give = lax.dynamic_index_in_dim(give_plan, partner, 0, keepdims=False)
    kept = (jnp.arange(tok, dtype=jnp.int32) < tok - own_give)[:, None]
    taken = (jnp.arange(GIVE, dtype=jnp.int32) >= GIVE - other_give)[:, None]

    def place(own, got):
        zero = jnp.zeros((), own.dtype)
        return jnp.concatenate([jnp.where(kept, own, zero), jnp.where(taken, got, zero)], axis=0)

    return (place(att, got_att), place(dq, got_dq), dwk, dwv)


def solution(mesh):
    return jax.shard_map(
        local,
        mesh=mesh,
        in_specs=(
            P("seq", "head"),
            P("seq", "head"),
            P("seq", "head"),
            P("seq", "head"),
            P("seq", "head"),
            P(),
            P(),
        ),
        out_specs=(P("seq", "head"), P("seq", "head"), P("seq", "head"), P("seq", "head")),
        check_vma=False,
    )
```

```python
import functools

import jax
import jax.numpy as jnp
from jax import lax
from jax.experimental import pallas as pl
from jax.experimental.pallas import tpu as pltpu
from jax.sharding import PartitionSpec as P

HD = 128
GROUP = 4
GIVE = 128
QUAD = 4
MESH = pl.DeviceIdType.MESH
F32 = jnp.float32
BF16 = jnp.bfloat16


def greet(peers, along):
    z, chain, above, below, head = along
    barrier = pltpu.get_barrier_semaphore()

    def call(peer):
        pl.semaphore_signal(barrier, inc=1, device_id=peer, device_id_type=MESH)

    for peer in peers:
        call(peer)

    @pl.when(z < chain - 1)
    def _():
        call((above, head))

    @pl.when(z > 0)
    def _():
        call((below, head))

    near = jnp.where(z < chain - 1, 1, 0) + jnp.where(z > 0, 1, 0)
    pl.semaphore_wait(barrier, len(peers) + near)


def remote(src, dst, send, recv, device):
    return pltpu.make_async_remote_copy(
        src_ref=src, dst_ref=dst, send_sem=send, recv_sem=recv, device_id=device, device_id_type=MESH
    )


def project_kernel(
    chain, heads,
    st_ref, wk_ref, wv_ref,
    keys_ref, values_ref, turned_ref,
    st_all, w_all, acc,
    st_send, st_recv, u_send, d_send, z_recv, y_send, y_recv, c_send, c_recv, own_sem, st_own_sem,
):
    seq = lax.axis_index("seq")
    head = lax.axis_index("head")
    z, quad = seq // QUAD, seq % QUAD
    base = z * QUAD
    other_y = base + (quad + 2) % 4
    other_c = base + (quad // 2) * 2 + (quad + 1) % 2
    rows, cols = wk_ref.shape
    wide = QUAD * rows
    pieces = st_ref.shape[1] // wide
    h_peers = [(head + k) % heads for k in range(1, heads)]
    above, below = seq + QUAD, seq - QUAD
    greet([(other_y, head), (other_c, head)] + [(seq, p) for p in h_peers], along=(z, chain, above, below, head))

    def rows_of(zz, qq):
        return pl.ds(pl.multiple_of((zz * QUAD + qq) * rows, rows), rows)

    def half(ref, at, side):
        return ref.at[at, pl.ds(side * cols, cols)]

    mate = (quad // 2) * 2 + (quad + 1) % 2
    sides = ((0, wk_ref), (1, wv_ref))

    def block(zz, qq, side):
        return half(w_all, rows_of(zz, qq), side)

    def up_copy(zz, side, src=None):
        at = block(zz, quad, side)
        return remote(at if src is None else src, at, u_send.at[zz, side], z_recv.at[zz, side], (above, head))

    def down_copy(zz, side, src=None):
        at = block(zz, quad, side)
        return remote(at if src is None else src, at, d_send.at[zz, side], z_recv.at[zz, side], (below, head))

    def y_copy(zz, side, src=None):
        at = block(zz, quad, side)
        return remote(at if src is None else src, at, y_send.at[zz, side], y_recv.at[zz, side], (other_y, head))

    def c_copy(zz, far, side, src=None):
        at = block(zz, (quad + 2 * far) % QUAD, side)
        return remote(
            at if src is None else src, at, c_send.at[zz, far, side], c_recv.at[zz, far, side], (other_c, head)
        )

    def y_wait(zz, side):
        at = block(zz, (quad + 2) % QUAD, side)
        remote(at, at, y_send.at[zz, side], y_recv.at[zz, side], (other_y, head)).wait_recv()

    def c_wait(zz, far, side):
        at = block(zz, (mate + 2 * far) % QUAD, side)
        remote(at, at, c_send.at[zz, far, side], c_recv.at[zz, far, side], (other_c, head)).wait_recv()

    for side, src in sides:
        y_copy(z, side, src).start()

        @pl.when(z < chain - 1)
        def _():
            up_copy(z, side, src).start()

        @pl.when(z > 0)
        def _():
            down_copy(z, side, src).start()

        c_copy(z, 0, side, src).start()
    own = []
    sent = []
    for n in range(pieces):
        part = st_ref.at[:, pl.ds(n * wide, wide)]
        for k in range(1, heads):
            copy = remote(
                part, st_all.at[head * pieces + n], st_send.at[k, n], st_recv.at[k, n], (seq, h_peers[k - 1])
            )
            copy.start()
            sent.append(copy)
        own.append(pltpu.make_async_copy(part, st_all.at[head * pieces + n], st_own_sem.at[n]))
    for side, src in sides:
        own.append(pltpu.make_async_copy(src, block(z, quad, side), own_sem.at[side]))
    for copy in own:
        copy.start()
    for copy in own:
        copy.wait()

    def turn(slot):
        flipped = st_all[slot].T
        for q in range(QUAD):
            turned_ref[q, pl.ds(pl.multiple_of(slot * rows, rows), rows), :] = flipped[q * rows:(q + 1) * rows, :]

    def arrive_z(zz, upward):
        for side in range(2):
            if upward:
                up_copy(zz, side).wait_recv()

                @pl.when(z < chain - 1)
                def _():
                    up_copy(zz, side).start()
            else:
                down_copy(zz, side).wait_recv()

                @pl.when(z > 0)
                def _():
                    down_copy(zz, side).start()
            y_copy(zz, side).start()
            c_copy(zz, 0, side).start()

    def arrive_y(zz):
        for side in range(2):
            y_wait(zz, side)
            c_copy(zz, 1, side).start()

    tile = min(2 * cols, 256)

    def multiply(zz, first=False):
        for far in range(2):
            for side in range(2):
                c_wait(zz, far, side)
        at = pl.ds(pl.multiple_of(zz * wide, wide), wide)

        def step(t, carry):
            where = pl.ds(pl.multiple_of(t * tile, tile), tile)
            term = jnp.dot(st_all[zz], w_all[at, where], preferred_element_type=F32)
            if first:
                acc[:, where] = term
            else:
                acc[:, where] += term
            return carry

        lax.fori_loop(0, 2 * cols // tile, step, 0)

    def sources(k):
        if k == 0:
            return [(z, None, None)]
        return [(z - k, z >= k, True), (z + k, z + k < chain, False)]

    def each(k, body):
        if not 0 <= k < chain:
            return
        for zz, there, upward in sources(k):
            if there is None:
                body(zz, upward)
            else:
                pl.when(there)(functools.partial(body, zz, upward))

    for k in range(chain + 2):
        if k:
            each(k, arrive_z)
        if k == 1:
            for n in range(pieces):
                turn(head * pieces + n)
        if k == min(2, chain - 1):
            for m in range(1, heads):
                for n in range(pieces):
                    slot = ((head - m + heads) % heads) * pieces + n
                    dst = st_all.at[slot]
                    remote(dst, dst, st_send.at[m, n], st_recv.at[m, n], (seq, h_peers[m - 1])).wait_recv()
                    turn(slot)
        each(k - 1, lambda zz, upward: arrive_y(zz))
        if k >= 2:
            each(k - 2, lambda zz, upward: multiply(zz, k == 2))
    keys_ref[...] = acc[:, :cols].astype(BF16)
    values_ref[...] = acc[:, cols:].astype(BF16)
    for copy in sent:
        copy.wait_send()
    for zz in range(chain):
        for side in range(2):
            y_copy(zz, side).wait_send()
            for far in range(2):
                c_copy(zz, far, side).wait_send()

            @pl.when((zz <= z) & (z < chain - 1))
            def _():
                up_copy(zz, side).wait_send()

            @pl.when((zz >= z) & (z > 0))
            def _():
                down_copy(zz, side).wait_send()


def attend_kernel(
    chain,
    turned_ref, q_ref, go_ref, keys_ref, values_ref, seg_row, seg_col,
    att_ref, dq_ref, got_att, got_dq, dwk_ref, dwv_ref,
    group_states, pair, terms, sums, ups, downs,
    s_send, s_recv, p_send, p_recv, u_send, u_recv, d_send, d_recv, h_send, h_recv, own_sem,
):
    seq = lax.axis_index("seq")
    head = lax.axis_index("head")
    z, quad = seq // QUAD, seq % QUAD
    base = z * QUAD
    tok = q_ref.shape[0]
    kv = keys_ref.shape[1] // HD
    rows = dwk_ref.shape[0]
    scale = HD ** (-0.5)
    across = ((z + chain // 2) % chain) * QUAD + quad
    above, below = seq + QUAD, seq - QUAD
    quads = [(quad + i) % QUAD for i in range(QUAD)]
    greet(
        [(across, head)] + [(base + p, head) for p in quads[1:]], along=(z, chain, above, below, head)
    )

    def span(i):
        return pl.ds(pl.multiple_of(i * tok, tok), tok)

    def states_copy(i):
        return remote(
            turned_ref.at[quads[i]], group_states.at[:, span(quad)],
            s_send.at[i], s_recv.at[i], (base + quads[i], head),
        )

    for i in range(1, QUAD):
        states_copy(i).start()
    own = pltpu.make_async_copy(turned_ref.at[quad], group_states.at[:, span(quad)], own_sem)
    own.start()
    own.wait()

    def pair_copy(g, i):
        return remote(
            pair.at[g, span(quad), :], pair.at[g, span(quad), :],
            p_send.at[g, i], p_recv.at[g, i], (base + quads[i], head),
        )

    def tail_copy(g, which):
        ref, dst = ((att_ref, got_att), (dq_ref, got_dq))[which]
        at = pl.ds(pl.multiple_of(g * (GROUP * HD), GROUP * HD), GROUP * HD)
        return remote(
            ref.at[pl.ds(tok - GIVE, GIVE), at], dst.at[:, at],
            h_send.at[g, which], h_recv.at[g, which], (across, head),
        )

    def rows_of(d):
        return pl.ds(d * rows, rows)

    def up_copy(g, d):
        return remote(
            sums.at[g, rows_of(d), :], ups.at[g, rows_of(d), :], u_send.at[g, d], u_recv.at[g, d], (above, head)
        )

    def down_copy(g, d):
        return remote(
            sums.at[g, rows_of(d), :], downs.at[g, rows_of(d), :], d_send.at[g, d], d_recv.at[g, d], (below, head)
        )

    places_r = lax.broadcasted_iota(jnp.int32, (tok, tok), 0)
    places_c = lax.broadcasted_iota(jnp.int32, (tok, tok), 1)
    allowed = (seg_row[...] == seg_col[...]) & (places_c <= places_r)
    nt = (((1,), (1,)), ((), ()))
    tn = (((0,), (0,)), ((), ()))

    def attend(g):
        at = pl.ds(pl.multiple_of(g * HD, HD), HD)
        key, value = keys_ref[:, at], values_ref[:, at]
        dk = dv = None
        for m in range(GROUP):
            col = pl.ds(pl.multiple_of(g * (GROUP * HD) + m * HD, HD), HD)
            query, grad = q_ref[:, col], go_ref[:, col]
            scores = lax.dot_general(query, key, nt, preferred_element_type=F32) * scale
            scores = jnp.where(allowed, scores, F32(-1e30))
            top = jnp.max(scores, axis=-1, keepdims=True)
            grown = jnp.exp(scores - top)
            probs = grown / jnp.sum(grown, axis=-1, keepdims=True)
            low = probs.astype(BF16)
            out = jnp.dot(low, value, preferred_element_type=F32).astype(BF16)
            att_ref[:, col] = out
            grad_probs = lax.dot_general(grad, value, nt, preferred_element_type=F32)
            dots = jnp.sum(grad.astype(F32) * out.astype(F32), axis=-1, keepdims=True)
            slope = (probs * (grad_probs - dots)).astype(BF16)
            dq = jnp.dot(slope, key, preferred_element_type=F32) * scale
            dq_ref[:, col] = dq.astype(BF16)
            dk_m = lax.dot_general(slope, query, tn, preferred_element_type=F32)
            dv_m = lax.dot_general(low, grad, tn, preferred_element_type=F32)
            dk = dk_m if dk is None else dk + dk_m
            dv = dv_m if dv is None else dv + dv_m
        pair[g, span(quad), pl.ds(0, HD)] = (dk * scale).astype(BF16)
        pair[g, span(quad), pl.ds(HD, HD)] = dv.astype(BF16)
        for i in range(1, QUAD):
            pair_copy(g, i).start()
        for which in range(2):
            tail_copy(g, which).start()

    def reduce(g):
        for i in range(1, QUAD):
            pair_copy(g, i).wait_recv()
        terms[g] = jnp.dot(group_states[...], pair[g], preferred_element_type=F32)
        if chain > 1:
            @pl.when(z == 0)
            def _():
                sums[g] = terms[g].astype(BF16)
                for d in range(chain - 1, 0, -1):
                    up_copy(g, d).start()

            @pl.when(z == chain - 1)
            def _():
                sums[g] = terms[g].astype(BF16)
                for d in range(chain - 1):
                    down_copy(g, d).start()

    def pass_on(g):
        for k in range(chain - 1):
            for d, there, copy, parts in (
                (chain - 1 - k, (z > 0) & (z < chain - 1 - k), up_copy, ups),
                (k, (z < chain - 1) & (z > k), down_copy, downs),
            ):
                @pl.when(there)
                def _():
                    copy(g, d).wait_recv()
                    mixed = terms[g, rows_of(d), :] + parts[g, rows_of(d), :].astype(F32)
                    sums[g, rows_of(d), :] = mixed.astype(BF16)
                    copy(g, d).start()

    def finish(g):
        for d in range(chain):
            @pl.when(z == d)
            def _():
                value = terms[g, rows_of(d), :]
                if d > 0:
                    up_copy(g, d).wait_recv()
                    value = value + ups[g, rows_of(d), :].astype(F32)
                if d < chain - 1:
                    down_copy(g, d).wait_recv()
                    value = value + downs[g, rows_of(d), :].astype(F32)
                dwk_ref[:, pl.ds(g * HD, HD)] = value[:, :HD]
                dwv_ref[:, pl.ds(g * HD, HD)] = value[:, HD:]

    def step(g, carry):
        @pl.when(g < kv)
        def _():
            attend(g)

        @pl.when(g == 1)
        def _():
            for i in range(1, QUAD):
                states_copy(i).wait_recv()

        @pl.when(g > 0)
        def _():
            reduce(g - 1)

        return carry

    lax.fori_loop(0, kv + 1, step, 0)
    for g in range(kv):
        pass_on(g)
    for g in range(kv):
        finish(g)
    for g in range(kv):
        for which in range(2):
            tail_copy(g, which).wait()
        for i in range(1, QUAD):
            pair_copy(g, i).wait_send()
        for d in range(chain):
            @pl.when(z < d)
            def _():
                up_copy(g, d).wait_send()

            @pl.when(z > d)
            def _():
                down_copy(g, d).wait_send()
    for i in range(1, QUAD):
        states_copy(i).wait_send()


def segment_ids(row_lengths, row_total):
    doc_ends = jnp.cumsum(row_lengths)
    places = jnp.arange(row_total, dtype=jnp.int32)
    return jnp.sum((places[:, None] >= doc_ends[None, :]).astype(jnp.int32), axis=1)


def local(states, queries, w_key, w_value, grad_out, lengths, give_plan):
    count, heads = lax.axis_size("seq"), lax.axis_size("head")
    chain = count // QUAD
    shard = lax.axis_index("seq")
    partner = jnp.bitwise_xor(shard, count // 2)
    tok = states.shape[0]
    rows, cols = w_key.shape
    kv = cols // HD
    deep = rows * count
    pieces = states.shape[1] // (QUAD * rows)
    vmem = pl.BlockSpec(memory_space=pltpu.VMEM)
    dma = pltpu.SemaphoreType.DMA
    limit = 56 * 2**20
    keys, values, turned = pl.pallas_call(
        functools.partial(project_kernel, chain, heads),
        out_shape=(
            jax.ShapeDtypeStruct((tok, cols), BF16),
            jax.ShapeDtypeStruct((tok, cols), BF16),
            jax.ShapeDtypeStruct((QUAD, chain * rows, tok), BF16),
        ),
        in_specs=[vmem] * 3,
        out_specs=(vmem,) * 3,
        scratch_shapes=[
            pltpu.VMEM((chain, tok, QUAD * rows), BF16),
            pltpu.VMEM((deep, 2 * cols), BF16),
            pltpu.VMEM((tok, 2 * cols), F32),
            dma((heads, pieces)), dma((heads, pieces)),
            dma((chain, 2)), dma((chain, 2)), dma((chain, 2)),
            dma((chain, 2)), dma((chain, 2)),
            dma((chain, 2, 2)), dma((chain, 2, 2)),
            dma((2,)), dma((pieces,)),
        ],
        compiler_params=pltpu.CompilerParams(
            collective_id=0, has_side_effects=True, vmem_limit_bytes=limit
        ),
        name="project",
    )(states, w_key, w_value)
    segment = segment_ids(lax.dynamic_index_in_dim(lengths, shard, 0, keepdims=False), tok)
    att, dq, got_att, got_dq, dwk, dwv = pl.pallas_call(
        functools.partial(attend_kernel, chain),
        out_shape=(
            jax.ShapeDtypeStruct(queries.shape, BF16),
            jax.ShapeDtypeStruct(queries.shape, BF16),
            jax.ShapeDtypeStruct((GIVE, queries.shape[1]), BF16),
            jax.ShapeDtypeStruct((GIVE, queries.shape[1]), BF16),
            jax.ShapeDtypeStruct((rows, cols), F32),
            jax.ShapeDtypeStruct((rows, cols), F32),
        ),
        in_specs=[vmem] * 7,
        out_specs=(vmem,) * 6,
        scratch_shapes=[
            pltpu.VMEM((chain * rows, QUAD * tok), BF16),
            pltpu.VMEM((kv, QUAD * tok, 2 * HD), BF16),
            pltpu.VMEM((kv, chain * rows, 2 * HD), F32),
            pltpu.VMEM((kv, chain * rows, 2 * HD), BF16),
            pltpu.VMEM((kv, chain * rows, 2 * HD), BF16),
            pltpu.VMEM((kv, chain * rows, 2 * HD), BF16),
            dma((QUAD,)), dma((QUAD,)),
            dma((kv, QUAD)), dma((kv, QUAD)),
            dma((kv, chain)), dma((kv, chain)),
            dma((kv, chain)), dma((kv, chain)),
            dma((kv, 2)), dma((kv, 2)),
            dma,
        ],
        compiler_params=pltpu.CompilerParams(
            collective_id=1, has_side_effects=True, vmem_limit_bytes=limit
        ),
        name="attend",
    )(turned, queries, grad_out, keys, values, segment[:, None], segment[None, :])
    own_give = lax.dynamic_index_in_dim(give_plan, shard, 0, keepdims=False)
    other_give = lax.dynamic_index_in_dim(give_plan, partner, 0, keepdims=False)
    kept = (jnp.arange(tok, dtype=jnp.int32) < tok - own_give)[:, None]
    taken = (jnp.arange(GIVE, dtype=jnp.int32) >= GIVE - other_give)[:, None]

    def place(own, got):
        zero = jnp.zeros((), own.dtype)
        return jnp.concatenate([jnp.where(kept, own, zero), jnp.where(taken, got, zero)], axis=0)

    return (place(att, got_att), place(dq, got_dq), dwk, dwv)


def solution(mesh):
    return jax.shard_map(
        local,
        mesh=mesh,
        in_specs=(
            P("seq", "head"),
            P("seq", "head"),
            P("seq", "head"),
            P("seq", "head"),
            P("seq", "head"),
            P(),
            P(),
        ),
        out_specs=(P("seq", "head"), P("seq", "head"), P("seq", "head"), P("seq", "head")),
        check_vma=False,
    )
```

```python
import functools

import jax
import jax.numpy as jnp
from jax import lax
from jax.experimental import pallas as pl
from jax.experimental.pallas import tpu as pltpu
from jax.sharding import PartitionSpec as P

HD = 128
GROUP = 4
GIVE = 128
QUAD = 4
MESH = pl.DeviceIdType.MESH
F32 = jnp.float32
BF16 = jnp.bfloat16


def greet(peers, along):
    z, chain, above, below, head = along
    barrier = pltpu.get_barrier_semaphore()

    def call(peer):
        pl.semaphore_signal(barrier, inc=1, device_id=peer, device_id_type=MESH)

    for peer in peers:
        call(peer)

    @pl.when(z < chain - 1)
    def _():
        call((above, head))

    @pl.when(z > 0)
    def _():
        call((below, head))

    near = jnp.where(z < chain - 1, 1, 0) + jnp.where(z > 0, 1, 0)
    pl.semaphore_wait(barrier, len(peers) + near)


def remote(src, dst, send, recv, device):
    return pltpu.make_async_remote_copy(
        src_ref=src, dst_ref=dst, send_sem=send, recv_sem=recv, device_id=device, device_id_type=MESH
    )


def project_kernel(
    chain, heads,
    st_ref, wk_ref, wv_ref,
    keys_ref, values_ref, turned_ref,
    st_all, w_all, acc,
    st_send, st_recv, u_send, d_send, z_recv, y_send, y_recv, c_send, c_recv, own_sem, st_own_sem,
):
    seq = lax.axis_index("seq")
    head = lax.axis_index("head")
    z, quad = seq // QUAD, seq % QUAD
    base = z * QUAD
    other_y = base + (quad + 2) % 4
    other_c = base + (quad // 2) * 2 + (quad + 1) % 2
    rows, cols = wk_ref.shape
    wide = QUAD * rows
    pieces = st_ref.shape[1] // wide
    h_peers = [(head + k) % heads for k in range(1, heads)]
    above, below = seq + QUAD, seq - QUAD
    greet([(other_y, head), (other_c, head)] + [(seq, p) for p in h_peers], along=(z, chain, above, below, head))

    def rows_of(zz, qq):
        return pl.ds(pl.multiple_of((zz * QUAD + qq) * rows, rows), rows)

    def half(ref, at, side):
        return ref.at[at, pl.ds(side * cols, cols)]

    mate = (quad // 2) * 2 + (quad + 1) % 2
    sides = ((0, wk_ref), (1, wv_ref))

    def block(zz, qq, side):
        return half(w_all, rows_of(zz, qq), side)

    def up_copy(zz, side, src=None):
        at = block(zz, quad, side)
        return remote(at if src is None else src, at, u_send.at[zz, side], z_recv.at[zz, side], (above, head))

    def down_copy(zz, side, src=None):
        at = block(zz, quad, side)
        return remote(at if src is None else src, at, d_send.at[zz, side], z_recv.at[zz, side], (below, head))

    def y_copy(zz, side, src=None):
        at = block(zz, quad, side)
        return remote(at if src is None else src, at, y_send.at[zz, side], y_recv.at[zz, side], (other_y, head))

    def c_copy(zz, far, side, src=None):
        at = block(zz, (quad + 2 * far) % QUAD, side)
        return remote(
            at if src is None else src, at, c_send.at[zz, far, side], c_recv.at[zz, far, side], (other_c, head)
        )

    def y_wait(zz, side):
        at = block(zz, (quad + 2) % QUAD, side)
        remote(at, at, y_send.at[zz, side], y_recv.at[zz, side], (other_y, head)).wait_recv()

    def c_wait(zz, far, side):
        at = block(zz, (mate + 2 * far) % QUAD, side)
        remote(at, at, c_send.at[zz, far, side], c_recv.at[zz, far, side], (other_c, head)).wait_recv()

    for side, src in sides:
        y_copy(z, side, src).start()

        @pl.when(z < chain - 1)
        def _():
            up_copy(z, side, src).start()

        @pl.when(z > 0)
        def _():
            down_copy(z, side, src).start()

        c_copy(z, 0, side, src).start()
    own = []
    sent = []
    for n in range(pieces):
        part = st_ref.at[:, pl.ds(n * wide, wide)]
        for k in range(1, heads):
            copy = remote(
                part, st_all.at[head * pieces + n], st_send.at[k, n], st_recv.at[k, n], (seq, h_peers[k - 1])
            )
            copy.start()
            sent.append(copy)
        own.append(pltpu.make_async_copy(part, st_all.at[head * pieces + n], st_own_sem.at[n]))
    for side, src in sides:
        own.append(pltpu.make_async_copy(src, block(z, quad, side), own_sem.at[side]))
    for copy in own:
        copy.start()
    for copy in own:
        copy.wait()

    def turn(slot):
        flipped = st_all[slot].T
        for q in range(QUAD):
            turned_ref[q, pl.ds(pl.multiple_of(slot * rows, rows), rows), :] = flipped[q * rows:(q + 1) * rows, :]

    def arrive_z(zz, upward):
        for side in range(2):
            if upward:
                up_copy(zz, side).wait_recv()

                @pl.when(z < chain - 1)
                def _():
                    up_copy(zz, side).start()
            else:
                down_copy(zz, side).wait_recv()

                @pl.when(z > 0)
                def _():
                    down_copy(zz, side).start()
            y_copy(zz, side).start()
            c_copy(zz, 0, side).start()

    def arrive_y(zz):
        for side in range(2):
            y_wait(zz, side)
            c_copy(zz, 1, side).start()

    tile = min(2 * cols, 256)

    def multiply(zz, first=False):
        for far in range(2):
            for side in range(2):
                c_wait(zz, far, side)
        at = pl.ds(pl.multiple_of(zz * wide, wide), wide)

        def step(t, carry):
            where = pl.ds(pl.multiple_of(t * tile, tile), tile)
            term = jnp.dot(st_all[zz], w_all[at, where], preferred_element_type=F32)
            if first:
                acc[:, where] = term
            else:
                acc[:, where] += term
            return carry

        lax.fori_loop(0, 2 * cols // tile, step, 0)

    def sources(k):
        if k == 0:
            return [(z, None, None)]
        return [(z - k, z >= k, True), (z + k, z + k < chain, False)]

    def each(k, body):
        if not 0 <= k < chain:
            return
        for zz, there, upward in sources(k):
            if there is None:
                body(zz, upward)
            else:
                pl.when(there)(functools.partial(body, zz, upward))

    for k in range(chain + 2):
        if k:
            each(k, arrive_z)
        if k == 1:
            for n in range(pieces):
                turn(head * pieces + n)
        if k == min(2, chain - 1):
            for m in range(1, heads):
                for n in range(pieces):
                    slot = ((head - m + heads) % heads) * pieces + n
                    dst = st_all.at[slot]
                    remote(dst, dst, st_send.at[m, n], st_recv.at[m, n], (seq, h_peers[m - 1])).wait_recv()
                    turn(slot)
        each(k - 1, lambda zz, upward: arrive_y(zz))
        if k >= 2:
            each(k - 2, lambda zz, upward: multiply(zz, k == 2))
    keys_ref[...] = acc[:, :cols].astype(BF16)
    values_ref[...] = acc[:, cols:].astype(BF16)
    for copy in sent:
        copy.wait_send()
    for zz in range(chain):
        for side in range(2):
            y_copy(zz, side).wait_send()
            for far in range(2):
                c_copy(zz, far, side).wait_send()

            @pl.when((zz <= z) & (z < chain - 1))
            def _():
                up_copy(zz, side).wait_send()

            @pl.when((zz >= z) & (z > 0))
            def _():
                down_copy(zz, side).wait_send()


def attend_kernel(
    chain,
    turned_ref, q_ref, go_ref, keys_ref, values_ref, seg_row, seg_col,
    att_ref, dq_ref, got_att, got_dq, dwk_ref, dwv_ref,
    group_states, pair, terms, sums, ups, downs,
    s_send, s_recv, p_send, p_recv, u_send, u_recv, d_send, d_recv, h_send, h_recv, own_sem,
):
    seq = lax.axis_index("seq")
    head = lax.axis_index("head")
    z, quad = seq // QUAD, seq % QUAD
    base = z * QUAD
    tok = q_ref.shape[0]
    kv = keys_ref.shape[1] // HD
    rows = dwk_ref.shape[0]
    scale = HD ** (-0.5)
    across = ((z + chain // 2) % chain) * QUAD + quad
    above, below = seq + QUAD, seq - QUAD
    quads = [(quad + i) % QUAD for i in range(QUAD)]
    greet(
        [(across, head)] + [(base + p, head) for p in quads[1:]], along=(z, chain, above, below, head)
    )

    def span(i):
        return pl.ds(pl.multiple_of(i * tok, tok), tok)

    def states_copy(i):
        return remote(
            turned_ref.at[quads[i]], group_states.at[:, span(quad)],
            s_send.at[i], s_recv.at[i], (base + quads[i], head),
        )

    for i in range(1, QUAD):
        states_copy(i).start()
    own = pltpu.make_async_copy(turned_ref.at[quad], group_states.at[:, span(quad)], own_sem)
    own.start()
    own.wait()

    def pair_copy(g, i):
        return remote(
            pair.at[g, span(quad), :], pair.at[g, span(quad), :],
            p_send.at[g, i], p_recv.at[g, i], (base + quads[i], head),
        )

    def tail_copy(g, m, which):
        ref, dst = ((att_ref, got_att), (dq_ref, got_dq))[which]
        at = pl.ds(pl.multiple_of(g * (GROUP * HD) + m * HD, HD), HD)
        return remote(
            ref.at[pl.ds(tok - GIVE, GIVE), at], dst.at[:, at],
            h_send.at[g, m, which], h_recv.at[g, m, which], (across, head),
        )

    def rows_of(d):
        return pl.ds(d * rows, rows)

    def up_copy(g, d):
        return remote(
            sums.at[g, rows_of(d), :], ups.at[g, rows_of(d), :], u_send.at[g, d], u_recv.at[g, d], (above, head)
        )

    def down_copy(g, d):
        return remote(
            sums.at[g, rows_of(d), :], downs.at[g, rows_of(d), :], d_send.at[g, d], d_recv.at[g, d], (below, head)
        )

    places_r = lax.broadcasted_iota(jnp.int32, (tok, tok), 0)
    places_c = lax.broadcasted_iota(jnp.int32, (tok, tok), 1)
    allowed = (seg_row[...] == seg_col[...]) & (places_c <= places_r)
    nt = (((1,), (1,)), ((), ()))
    tn = (((0,), (0,)), ((), ()))

    def attend(g):
        at = pl.ds(pl.multiple_of(g * HD, HD), HD)
        key, value = keys_ref[:, at], values_ref[:, at]
        dk = dv = None
        for m in range(GROUP):
            col = pl.ds(pl.multiple_of(g * (GROUP * HD) + m * HD, HD), HD)
            query, grad = q_ref[:, col], go_ref[:, col]
            scores = lax.dot_general(query, key, nt, preferred_element_type=F32) * scale
            scores = jnp.where(allowed, scores, F32(-1e30))
            top = jnp.max(scores, axis=-1, keepdims=True)
            grown = jnp.exp(scores - top)
            probs = grown / jnp.sum(grown, axis=-1, keepdims=True)
            low = probs.astype(BF16)
            out = jnp.dot(low, value, preferred_element_type=F32).astype(BF16)
            att_ref[:, col] = out
            grad_probs = lax.dot_general(grad, value, nt, preferred_element_type=F32)
            dots = jnp.sum(grad.astype(F32) * out.astype(F32), axis=-1, keepdims=True)
            slope = (probs * (grad_probs - dots)).astype(BF16)
            dq = jnp.dot(slope, key, preferred_element_type=F32) * scale
            dq_ref[:, col] = dq.astype(BF16)
            for which in range(2):
                tail_copy(g, m, which).start()
            dk_m = lax.dot_general(slope, query, tn, preferred_element_type=F32)
            dv_m = lax.dot_general(low, grad, tn, preferred_element_type=F32)
            dk = dk_m if dk is None else dk + dk_m
            dv = dv_m if dv is None else dv + dv_m
        pair[g, span(quad), pl.ds(0, HD)] = (dk * scale).astype(BF16)
        pair[g, span(quad), pl.ds(HD, HD)] = dv.astype(BF16)
        for i in range(1, QUAD):
            pair_copy(g, i).start()

    def reduce(g):
        for i in range(1, QUAD):
            pair_copy(g, i).wait_recv()
        terms[g] = jnp.dot(group_states[...], pair[g], preferred_element_type=F32)
        if chain > 1:
            @pl.when(z == 0)
            def _():
                sums[g] = terms[g].astype(BF16)
                for d in range(chain - 1, 0, -1):
                    up_copy(g, d).start()

            @pl.when(z == chain - 1)
            def _():
                sums[g] = terms[g].astype(BF16)
                for d in range(chain - 1):
                    down_copy(g, d).start()

    def pass_one(g, d, there, copy, parts):
        @pl.when(there)
        def _():
            copy(g, d).wait_recv()
            mixed = terms[g, rows_of(d), :] + parts[g, rows_of(d), :].astype(F32)
            sums[g, rows_of(d), :] = mixed.astype(BF16)
            copy(g, d).start()

    def pass_up(g):
        for d in range(chain - 1, 1, -1):
            pass_one(g, d, (z > 0) & (z < d), up_copy, ups)

    def pass_down(g):
        for d in range(chain - 2):
            pass_one(g, d, (z < chain - 1) & (z > d), down_copy, downs)

    low_side = z < chain // 2

    def pass_on(g, early):
        pl.when(low_side)(lambda: pass_up(g) if early else pass_down(g))
        pl.when(jnp.logical_not(low_side))(lambda: pass_down(g) if early else pass_up(g))

    def finish(g):
        for d in range(chain):
            @pl.when(z == d)
            def _():
                value = terms[g, rows_of(d), :]
                if d > 0:
                    up_copy(g, d).wait_recv()
                    value = value + ups[g, rows_of(d), :].astype(F32)
                if d < chain - 1:
                    down_copy(g, d).wait_recv()
                    value = value + downs[g, rows_of(d), :].astype(F32)
                dwk_ref[:, pl.ds(g * HD, HD)] = value[:, :HD]
                dwv_ref[:, pl.ds(g * HD, HD)] = value[:, HD:]

    def step(g, carry):
        @pl.when(g < kv)
        def _():
            attend(g)

        @pl.when(g == 1)
        def _():
            for i in range(1, QUAD):
                states_copy(i).wait_recv()

        @pl.when((g > 0) & (g < kv + 1))
        def _():
            reduce(g - 1)

        @pl.when((g > 1) & (g < kv + 2))
        def _():
            pass_on(g - 2, True)

        @pl.when(g > 2)
        def _():
            pass_on(g - 3, False)

        return carry

    lax.fori_loop(0, kv + 3, step, 0)
    for g in range(kv):
        finish(g)
    for g in range(kv):
        for m in range(GROUP):
            for which in range(2):
                tail_copy(g, m, which).wait()
        for i in range(1, QUAD):
            pair_copy(g, i).wait_send()
        for d in range(chain):
            @pl.when(z < d)
            def _():
                up_copy(g, d).wait_send()

            @pl.when(z > d)
            def _():
                down_copy(g, d).wait_send()
    for i in range(1, QUAD):
        states_copy(i).wait_send()


def segment_ids(row_lengths, row_total):
    doc_ends = jnp.cumsum(row_lengths)
    places = jnp.arange(row_total, dtype=jnp.int32)
    return jnp.sum((places[:, None] >= doc_ends[None, :]).astype(jnp.int32), axis=1)


def local(states, queries, w_key, w_value, grad_out, lengths, give_plan):
    count, heads = lax.axis_size("seq"), lax.axis_size("head")
    chain = count // QUAD
    shard = lax.axis_index("seq")
    partner = jnp.bitwise_xor(shard, count // 2)
    tok = states.shape[0]
    rows, cols = w_key.shape
    kv = cols // HD
    deep = rows * count
    pieces = states.shape[1] // (QUAD * rows)
    vmem = pl.BlockSpec(memory_space=pltpu.VMEM)
    dma = pltpu.SemaphoreType.DMA
    limit = 56 * 2**20
    keys, values, turned = pl.pallas_call(
        functools.partial(project_kernel, chain, heads),
        out_shape=(
            jax.ShapeDtypeStruct((tok, cols), BF16),
            jax.ShapeDtypeStruct((tok, cols), BF16),
            jax.ShapeDtypeStruct((QUAD, chain * rows, tok), BF16),
        ),
        in_specs=[vmem] * 3,
        out_specs=(vmem,) * 3,
        scratch_shapes=[
            pltpu.VMEM((chain, tok, QUAD * rows), BF16),
            pltpu.VMEM((deep, 2 * cols), BF16),
            pltpu.VMEM((tok, 2 * cols), F32),
            dma((heads, pieces)), dma((heads, pieces)),
            dma((chain, 2)), dma((chain, 2)), dma((chain, 2)),
            dma((chain, 2)), dma((chain, 2)),
            dma((chain, 2, 2)), dma((chain, 2, 2)),
            dma((2,)), dma((pieces,)),
        ],
        compiler_params=pltpu.CompilerParams(
            collective_id=0, has_side_effects=True, vmem_limit_bytes=limit
        ),
        name="project",
    )(states, w_key, w_value)
    segment = segment_ids(lax.dynamic_index_in_dim(lengths, shard, 0, keepdims=False), tok)
    att, dq, got_att, got_dq, dwk, dwv = pl.pallas_call(
        functools.partial(attend_kernel, chain),
        out_shape=(
            jax.ShapeDtypeStruct(queries.shape, BF16),
            jax.ShapeDtypeStruct(queries.shape, BF16),
            jax.ShapeDtypeStruct((GIVE, queries.shape[1]), BF16),
            jax.ShapeDtypeStruct((GIVE, queries.shape[1]), BF16),
            jax.ShapeDtypeStruct((rows, cols), F32),
            jax.ShapeDtypeStruct((rows, cols), F32),
        ),
        in_specs=[vmem] * 7,
        out_specs=(vmem,) * 6,
        scratch_shapes=[
            pltpu.VMEM((chain * rows, QUAD * tok), BF16),
            pltpu.VMEM((kv, QUAD * tok, 2 * HD), BF16),
            pltpu.VMEM((kv, chain * rows, 2 * HD), F32),
            pltpu.VMEM((kv, chain * rows, 2 * HD), BF16),
            pltpu.VMEM((kv, chain * rows, 2 * HD), BF16),
            pltpu.VMEM((kv, chain * rows, 2 * HD), BF16),
            dma((QUAD,)), dma((QUAD,)),
            dma((kv, QUAD)), dma((kv, QUAD)),
            dma((kv, chain)), dma((kv, chain)),
            dma((kv, chain)), dma((kv, chain)),
            dma((kv, GROUP, 2)), dma((kv, GROUP, 2)),
            dma,
        ],
        compiler_params=pltpu.CompilerParams(
            collective_id=1, has_side_effects=True, vmem_limit_bytes=limit
        ),
        name="attend",
    )(turned, queries, grad_out, keys, values, segment[:, None], segment[None, :])
    own_give = lax.dynamic_index_in_dim(give_plan, shard, 0, keepdims=False)
    other_give = lax.dynamic_index_in_dim(give_plan, partner, 0, keepdims=False)
    kept = (jnp.arange(tok, dtype=jnp.int32) < tok - own_give)[:, None]
    taken = (jnp.arange(GIVE, dtype=jnp.int32) >= GIVE - other_give)[:, None]

    def place(own, got):
        zero = jnp.zeros((), own.dtype)
        return jnp.concatenate([jnp.where(kept, own, zero), jnp.where(taken, got, zero)], axis=0)

    return (place(att, got_att), place(dq, got_dq), dwk, dwv)


def solution(mesh):
    return jax.shard_map(
        local,
        mesh=mesh,
        in_specs=(
            P("seq", "head"),
            P("seq", "head"),
            P("seq", "head"),
            P("seq", "head"),
            P("seq", "head"),
            P(),
            P(),
        ),
        out_specs=(P("seq", "head"), P("seq", "head"), P("seq", "head"), P("seq", "head")),
        check_vma=False,
    )
```

```python
import functools

import jax
import jax.numpy as jnp
from jax import lax
from jax.experimental import pallas as pl
from jax.experimental.pallas import tpu as pltpu
from jax.sharding import PartitionSpec as P

HD = 128
GROUP = 4
GIVE = 128
QUAD = 4
MESH = pl.DeviceIdType.MESH
F32 = jnp.float32
BF16 = jnp.bfloat16


def greet(peers, along):
    z, chain, above, below, head = along
    barrier = pltpu.get_barrier_semaphore()

    def call(peer):
        pl.semaphore_signal(barrier, inc=1, device_id=peer, device_id_type=MESH)

    for peer in peers:
        call(peer)

    @pl.when(z < chain - 1)
    def _():
        call((above, head))

    @pl.when(z > 0)
    def _():
        call((below, head))

    near = jnp.where(z < chain - 1, 1, 0) + jnp.where(z > 0, 1, 0)
    pl.semaphore_wait(barrier, len(peers) + near)


def remote(src, dst, send, recv, device):
    return pltpu.make_async_remote_copy(
        src_ref=src, dst_ref=dst, send_sem=send, recv_sem=recv, device_id=device, device_id_type=MESH
    )


def project_kernel(
    chain, heads,
    st_ref, wk_ref, wv_ref,
    keys_ref, values_ref, turned_ref,
    st_all, w_all, acc,
    st_send, st_recv, u_send, d_send, z_recv, y_send, y_recv, c_send, c_recv, own_sem, st_own_sem,
):
    seq = lax.axis_index("seq")
    head = lax.axis_index("head")
    z, quad = seq // QUAD, seq % QUAD
    base = z * QUAD
    other_y = base + (quad + 2) % 4
    other_c = base + (quad // 2) * 2 + (quad + 1) % 2
    rows, cols = wk_ref.shape
    wide = QUAD * rows
    pieces = st_ref.shape[1] // wide
    h_peers = [(head + k) % heads for k in range(1, heads)]
    above, below = seq + QUAD, seq - QUAD
    greet([(other_y, head), (other_c, head)] + [(seq, p) for p in h_peers], along=(z, chain, above, below, head))

    def rows_of(zz, qq):
        return pl.ds(pl.multiple_of((zz * QUAD + qq) * rows, rows), rows)

    def half(ref, at, side):
        return ref.at[at, pl.ds(side * cols, cols)]

    mate = (quad // 2) * 2 + (quad + 1) % 2
    sides = ((0, wk_ref), (1, wv_ref))

    def block(zz, qq, side):
        return half(w_all, rows_of(zz, qq), side)

    def up_copy(zz, side, src=None):
        at = block(zz, quad, side)
        return remote(at if src is None else src, at, u_send.at[zz, side], z_recv.at[zz, side], (above, head))

    def down_copy(zz, side, src=None):
        at = block(zz, quad, side)
        return remote(at if src is None else src, at, d_send.at[zz, side], z_recv.at[zz, side], (below, head))

    def y_copy(zz, side, src=None):
        at = block(zz, quad, side)
        return remote(at if src is None else src, at, y_send.at[zz, side], y_recv.at[zz, side], (other_y, head))

    def c_copy(zz, far, side, src=None):
        at = block(zz, (quad + 2 * far) % QUAD, side)
        return remote(
            at if src is None else src, at, c_send.at[zz, far, side], c_recv.at[zz, far, side], (other_c, head)
        )

    def y_wait(zz, side):
        at = block(zz, (quad + 2) % QUAD, side)
        remote(at, at, y_send.at[zz, side], y_recv.at[zz, side], (other_y, head)).wait_recv()

    def c_wait(zz, far, side):
        at = block(zz, (mate + 2 * far) % QUAD, side)
        remote(at, at, c_send.at[zz, far, side], c_recv.at[zz, far, side], (other_c, head)).wait_recv()

    for side, src in sides:
        y_copy(z, side, src).start()

        @pl.when(z < chain - 1)
        def _():
            up_copy(z, side, src).start()

        @pl.when(z > 0)
        def _():
            down_copy(z, side, src).start()

        c_copy(z, 0, side, src).start()
    own = []
    sent = []
    for n in range(pieces):
        part = st_ref.at[:, pl.ds(n * wide, wide)]
        for k in range(1, heads):
            copy = remote(
                part, st_all.at[head * pieces + n], st_send.at[k, n], st_recv.at[k, n], (seq, h_peers[k - 1])
            )
            copy.start()
            sent.append(copy)
        own.append(pltpu.make_async_copy(part, st_all.at[head * pieces + n], st_own_sem.at[n]))
    for side, src in sides:
        own.append(pltpu.make_async_copy(src, block(z, quad, side), own_sem.at[side]))
    for copy in own:
        copy.start()
    for copy in own:
        copy.wait()

    def turn(slot):
        flipped = st_all[slot].T
        for q in range(QUAD):
            turned_ref[q, pl.ds(pl.multiple_of(slot * rows, rows), rows), :] = flipped[q * rows:(q + 1) * rows, :]

    def arrive_z(zz, upward):
        for side in range(2):
            if upward:
                up_copy(zz, side).wait_recv()

                @pl.when(z < chain - 1)
                def _():
                    up_copy(zz, side).start()
            else:
                down_copy(zz, side).wait_recv()

                @pl.when(z > 0)
                def _():
                    down_copy(zz, side).start()
            y_copy(zz, side).start()
            c_copy(zz, 0, side).start()

    def arrive_y(zz):
        for side in range(2):
            y_wait(zz, side)
            c_copy(zz, 1, side).start()

    tile = min(2 * cols, 256)

    def multiply(zz, first=False):
        for far in range(2):
            for side in range(2):
                c_wait(zz, far, side)
        at = pl.ds(pl.multiple_of(zz * wide, wide), wide)

        def step(t, carry):
            where = pl.ds(pl.multiple_of(t * tile, tile), tile)
            term = jnp.dot(st_all[zz], w_all[at, where], preferred_element_type=F32)
            if first:
                acc[:, where] = term
            else:
                acc[:, where] += term
            return carry

        lax.fori_loop(0, 2 * cols // tile, step, 0)

    def sources(k):
        if k == 0:
            return [(z, None, None)]
        return [(z - k, z >= k, True), (z + k, z + k < chain, False)]

    def each(k, body):
        if not 0 <= k < chain:
            return
        for zz, there, upward in sources(k):
            if there is None:
                body(zz, upward)
            else:
                pl.when(there)(functools.partial(body, zz, upward))

    for k in range(chain + 2):
        if k:
            each(k, arrive_z)
        if k == 1:
            for n in range(pieces):
                turn(head * pieces + n)
        if k == min(2, chain - 1):
            for m in range(1, heads):
                for n in range(pieces):
                    slot = ((head - m + heads) % heads) * pieces + n
                    dst = st_all.at[slot]
                    remote(dst, dst, st_send.at[m, n], st_recv.at[m, n], (seq, h_peers[m - 1])).wait_recv()
                    turn(slot)
        each(k - 1, lambda zz, upward: arrive_y(zz))
        if k >= 2:
            each(k - 2, lambda zz, upward: multiply(zz, k == 2))
    keys_ref[...] = acc[:, :cols].astype(BF16)
    values_ref[...] = acc[:, cols:].astype(BF16)
    for copy in sent:
        copy.wait_send()
    for zz in range(chain):
        for side in range(2):
            y_copy(zz, side).wait_send()
            for far in range(2):
                c_copy(zz, far, side).wait_send()

            @pl.when((zz <= z) & (z < chain - 1))
            def _():
                up_copy(zz, side).wait_send()

            @pl.when((zz >= z) & (z > 0))
            def _():
                down_copy(zz, side).wait_send()


def attend_kernel(
    chain, heads,
    turned_ref, q_ref, go_ref, keys_ref, values_ref, seg_row, seg_col,
    att_ref, dq_ref, got_att, got_dq, dwk_ref, dwv_ref,
    group_states, pair, terms, sums, ups, downs,
    s_send, s_recv, x_send, x_recv, p_send, p_recv, u_send, u_recv, d_send, d_recv, h_send, h_recv, own_sem,
):
    seq = lax.axis_index("seq")
    head = lax.axis_index("head")
    z, quad = seq // QUAD, seq % QUAD
    base = z * QUAD
    tok = q_ref.shape[0]
    kv = keys_ref.shape[1] // HD
    rows = dwk_ref.shape[0]
    scale = HD ** (-0.5)
    across = ((z + chain // 2) % chain) * QUAD + quad
    above, below = seq + QUAD, seq - QUAD
    quads = [(quad + i) % QUAD for i in range(QUAD)]
    mate = (quad // 2) * 2 + (quad + 1) % 2
    h_peers = [(head + k) % heads for k in range(1, heads)]
    part = (chain // heads) * rows
    greet(
        [(across, head)] + [(base + p, head) for p in quads[1:]] + [(seq, p) for p in h_peers],
        along=(z, chain, above, below, head)
    )

    def span(i):
        return pl.ds(pl.multiple_of(i * tok, tok), tok)

    def share(hh):
        return pl.ds(pl.multiple_of(hh * part, part), part)

    def states_copy(i):
        return remote(
            turned_ref.at[quads[i], share(head), :], group_states.at[share(head), span(quad)],
            s_send.at[i], s_recv.at[i], (base + quads[i], head),
        )

    def share_copy(i, k, hh):
        at = group_states.at[share(hh), span((quad - i + QUAD) % QUAD)]
        return remote(at, at, x_send.at[i, k], x_recv.at[i, k], (seq, h_peers[k - 1]))

    for i in range(1, QUAD):
        states_copy(i).start()
    own = pltpu.make_async_copy(turned_ref.at[quad], group_states.at[:, span(quad)], own_sem)
    own.start()
    own.wait()

    def pair_copy(g, i):
        at = pair.at[g, span((quad + 2) % QUAD if i == 3 else quad), :]
        to = (quad + 2) % QUAD if i == 2 else mate
        return remote(at, at, p_send.at[g, i], p_recv.at[g, i], (base + to, head))

    def tail_copy(g, m, which):
        ref, dst = ((att_ref, got_att), (dq_ref, got_dq))[which]
        at = pl.ds(pl.multiple_of(g * (GROUP * HD) + m * HD, HD), HD)
        return remote(
            ref.at[pl.ds(tok - GIVE, GIVE), at], dst.at[:, at],
            h_send.at[g, m, which], h_recv.at[g, m, which], (across, head),
        )

    def rows_of(d):
        return pl.ds(d * rows, rows)

    def up_copy(g, d):
        return remote(
            sums.at[g, rows_of(d), :], ups.at[g, rows_of(d), :], u_send.at[g, d], u_recv.at[g, d], (above, head)
        )

    def down_copy(g, d):
        return remote(
            sums.at[g, rows_of(d), :], downs.at[g, rows_of(d), :], d_send.at[g, d], d_recv.at[g, d], (below, head)
        )

    places_r = lax.broadcasted_iota(jnp.int32, (tok, tok), 0)
    places_c = lax.broadcasted_iota(jnp.int32, (tok, tok), 1)
    allowed = (seg_row[...] == seg_col[...]) & (places_c <= places_r)
    nt = (((1,), (1,)), ((), ()))
    tn = (((0,), (0,)), ((), ()))

    def attend(g):
        at = pl.ds(pl.multiple_of(g * HD, HD), HD)
        key, value = keys_ref[:, at], values_ref[:, at]
        dk = dv = None
        for m in range(GROUP):
            col = pl.ds(pl.multiple_of(g * (GROUP * HD) + m * HD, HD), HD)
            query, grad = q_ref[:, col], go_ref[:, col]
            scores = lax.dot_general(query, key, nt, preferred_element_type=F32) * scale
            scores = jnp.where(allowed, scores, F32(-1e30))
            top = jnp.max(scores, axis=-1, keepdims=True)
            grown = jnp.exp(scores - top)
            probs = grown / jnp.sum(grown, axis=-1, keepdims=True)
            low = probs.astype(BF16)
            out = jnp.dot(low, value, preferred_element_type=F32).astype(BF16)
            att_ref[:, col] = out
            grad_probs = lax.dot_general(grad, value, nt, preferred_element_type=F32)
            dots = jnp.sum(grad.astype(F32) * out.astype(F32), axis=-1, keepdims=True)
            slope = (probs * (grad_probs - dots)).astype(BF16)
            dq = jnp.dot(slope, key, preferred_element_type=F32) * scale
            dq_ref[:, col] = dq.astype(BF16)
            for which in range(2):
                tail_copy(g, m, which).start()
            dk_m = lax.dot_general(slope, query, tn, preferred_element_type=F32)
            dv_m = lax.dot_general(low, grad, tn, preferred_element_type=F32)
            dk = dk_m if dk is None else dk + dk_m
            dv = dv_m if dv is None else dv + dv_m
        pair[g, span(quad), pl.ds(0, HD)] = (dk * scale).astype(BF16)
        pair[g, span(quad), pl.ds(HD, HD)] = dv.astype(BF16)
        pair_copy(g, 2).start()
        pair_copy(g, 1).start()

    def reduce(g):
        pair_copy(g, 1).wait_recv()
        pair_copy(g, 3).wait_recv()
        terms[g] = jnp.dot(group_states[...], pair[g], preferred_element_type=F32)
        if chain > 1:
            @pl.when(z == 0)
            def _():
                sums[g] = terms[g].astype(BF16)
                for d in range(chain - 1, 0, -1):
                    up_copy(g, d).start()

            @pl.when(z == chain - 1)
            def _():
                sums[g] = terms[g].astype(BF16)
                for d in range(chain - 1):
                    down_copy(g, d).start()

    def pass_one(g, d, there, copy, parts):
        @pl.when(there)
        def _():
            copy(g, d).wait_recv()
            mixed = terms[g, rows_of(d), :] + parts[g, rows_of(d), :].astype(F32)
            sums[g, rows_of(d), :] = mixed.astype(BF16)
            copy(g, d).start()

    def pass_up(g):
        for d in range(chain - 1, 1, -1):
            pass_one(g, d, (z > 0) & (z < d), up_copy, ups)

    def pass_down(g):
        for d in range(chain - 2):
            pass_one(g, d, (z < chain - 1) & (z > d), down_copy, downs)

    low_side = z < chain // 2

    def pass_on(g, early):
        pl.when(low_side)(lambda: pass_up(g) if early else pass_down(g))
        pl.when(jnp.logical_not(low_side))(lambda: pass_down(g) if early else pass_up(g))

    def finish(g):
        for d in range(chain):
            @pl.when(z == d)
            def _():
                value = terms[g, rows_of(d), :]
                if d > 0:
                    up_copy(g, d).wait_recv()
                    value = value + ups[g, rows_of(d), :].astype(F32)
                if d < chain - 1:
                    down_copy(g, d).wait_recv()
                    value = value + downs[g, rows_of(d), :].astype(F32)
                dwk_ref[:, pl.ds(g * HD, HD)] = value[:, :HD]
                dwv_ref[:, pl.ds(g * HD, HD)] = value[:, HD:]

    def step(g, carry):
        @pl.when(g < kv)
        def _():
            attend(g)

        @pl.when(g == 1)
        def _():
            for i in range(1, QUAD):
                states_copy(i).wait_recv()
                for k in range(1, heads):
                    share_copy(i, k, head).start()

        @pl.when((g > 0) & (g < kv + 1))
        def _():
            pair_copy(g - 1, 2).wait_recv()
            pair_copy(g - 1, 3).start()

        @pl.when(g == 2)
        def _():
            for i in range(1, QUAD):
                for k in range(1, heads):
                    share_copy(i, k, (head - k + heads) % heads).wait_recv()

        @pl.when((g > 1) & (g < kv + 2))
        def _():
            reduce(g - 2)

        @pl.when((g > 2) & (g < kv + 3))
        def _():
            pass_on(g - 3, True)

        @pl.when(g > 3)
        def _():
            pass_on(g - 4, False)

        return carry

    lax.fori_loop(0, kv + 4, step, 0)
    for g in range(kv):
        finish(g)
    for g in range(kv):
        for m in range(GROUP):
            for which in range(2):
                tail_copy(g, m, which).wait()
        for i in range(1, QUAD):
            pair_copy(g, i).wait_send()
        for d in range(chain):
            @pl.when(z < d)
            def _():
                up_copy(g, d).wait_send()

            @pl.when(z > d)
            def _():
                down_copy(g, d).wait_send()
    for i in range(1, QUAD):
        states_copy(i).wait_send()
        for k in range(1, heads):
            share_copy(i, k, head).wait_send()


def segment_ids(row_lengths, row_total):
    doc_ends = jnp.cumsum(row_lengths)
    places = jnp.arange(row_total, dtype=jnp.int32)
    return jnp.sum((places[:, None] >= doc_ends[None, :]).astype(jnp.int32), axis=1)


def local(states, queries, w_key, w_value, grad_out, lengths, give_plan):
    count, heads = lax.axis_size("seq"), lax.axis_size("head")
    chain = count // QUAD
    shard = lax.axis_index("seq")
    partner = jnp.bitwise_xor(shard, count // 2)
    tok = states.shape[0]
    rows, cols = w_key.shape
    kv = cols // HD
    deep = rows * count
    pieces = states.shape[1] // (QUAD * rows)
    vmem = pl.BlockSpec(memory_space=pltpu.VMEM)
    dma = pltpu.SemaphoreType.DMA
    limit = 56 * 2**20
    keys, values, turned = pl.pallas_call(
        functools.partial(project_kernel, chain, heads),
        out_shape=(
            jax.ShapeDtypeStruct((tok, cols), BF16),
            jax.ShapeDtypeStruct((tok, cols), BF16),
            jax.ShapeDtypeStruct((QUAD, chain * rows, tok), BF16),
        ),
        in_specs=[vmem] * 3,
        out_specs=(vmem,) * 3,
        scratch_shapes=[
            pltpu.VMEM((chain, tok, QUAD * rows), BF16),
            pltpu.VMEM((deep, 2 * cols), BF16),
            pltpu.VMEM((tok, 2 * cols), F32),
            dma((heads, pieces)), dma((heads, pieces)),
            dma((chain, 2)), dma((chain, 2)), dma((chain, 2)),
            dma((chain, 2)), dma((chain, 2)),
            dma((chain, 2, 2)), dma((chain, 2, 2)),
            dma((2,)), dma((pieces,)),
        ],
        compiler_params=pltpu.CompilerParams(
            collective_id=0, has_side_effects=True, vmem_limit_bytes=limit
        ),
        name="project",
    )(states, w_key, w_value)
    segment = segment_ids(lax.dynamic_index_in_dim(lengths, shard, 0, keepdims=False), tok)
    att, dq, got_att, got_dq, dwk, dwv = pl.pallas_call(
        functools.partial(attend_kernel, chain, heads),
        out_shape=(
            jax.ShapeDtypeStruct(queries.shape, BF16),
            jax.ShapeDtypeStruct(queries.shape, BF16),
            jax.ShapeDtypeStruct((GIVE, queries.shape[1]), BF16),
            jax.ShapeDtypeStruct((GIVE, queries.shape[1]), BF16),
            jax.ShapeDtypeStruct((rows, cols), F32),
            jax.ShapeDtypeStruct((rows, cols), F32),
        ),
        in_specs=[vmem] * 7,
        out_specs=(vmem,) * 6,
        scratch_shapes=[
            pltpu.VMEM((chain * rows, QUAD * tok), BF16),
            pltpu.VMEM((kv, QUAD * tok, 2 * HD), BF16),
            pltpu.VMEM((kv, chain * rows, 2 * HD), F32),
            pltpu.VMEM((kv, chain * rows, 2 * HD), BF16),
            pltpu.VMEM((kv, chain * rows, 2 * HD), BF16),
            pltpu.VMEM((kv, chain * rows, 2 * HD), BF16),
            dma((QUAD,)), dma((QUAD,)),
            dma((QUAD, heads)), dma((QUAD, heads)),
            dma((kv, QUAD)), dma((kv, QUAD)),
            dma((kv, chain)), dma((kv, chain)),
            dma((kv, chain)), dma((kv, chain)),
            dma((kv, GROUP, 2)), dma((kv, GROUP, 2)),
            dma,
        ],
        compiler_params=pltpu.CompilerParams(
            collective_id=1, has_side_effects=True, vmem_limit_bytes=limit
        ),
        name="attend",
    )(turned, queries, grad_out, keys, values, segment[:, None], segment[None, :])
    own_give = lax.dynamic_index_in_dim(give_plan, shard, 0, keepdims=False)
    other_give = lax.dynamic_index_in_dim(give_plan, partner, 0, keepdims=False)
    kept = (jnp.arange(tok, dtype=jnp.int32) < tok - own_give)[:, None]
    taken = (jnp.arange(GIVE, dtype=jnp.int32) >= GIVE - other_give)[:, None]

    def place(own, got):
        zero = jnp.zeros((), own.dtype)
        return jnp.concatenate([jnp.where(kept, own, zero), jnp.where(taken, got, zero)], axis=0)

    return (place(att, got_att), place(dq, got_dq), dwk, dwv)


def solution(mesh):
    return jax.shard_map(
        local,
        mesh=mesh,
        in_specs=(
            P("seq", "head"),
            P("seq", "head"),
            P("seq", "head"),
            P("seq", "head"),
            P("seq", "head"),
            P(),
            P(),
        ),
        out_specs=(P("seq", "head"), P("seq", "head"), P("seq", "head"), P("seq", "head")),
        check_vma=False,
    )
```
